32 devices in a mesh: dp: 4 (over z), mp: 8 (over y, x, core).
Axes of the slice: x: 2, y: 2, z: 4, core: 2. Of those that a mesh axis runs over, the one named last changes fastest.
Arguments:
- accumulated: bfloat16 [4, 14336, 4096], P('dp', 'mp'), may hold values from -6 to 6
- start_q: float32 [4096, 128], replicated, may hold values from -6 to 6
Outputs:
- update: float32 [14336, 4096], P('mp')
- new_error: bfloat16 [4, 14336, 4096], P('dp', 'mp')
The draws below stay inside these ranges and needn't reach their ends.
All inputs are finite; a program needn't handle non-finite values.
Results may differ from the reference program's by a relative error of at most 0.0059.
Values sent between devices are 32-bit elements; how exact they have to be, the bound alone decides.
A program may use at most 128 MiB of HBM per device.

```python
import jax
import jax.numpy as jnp
from jax import lax

D = 4096
HID = 14336
R = 128
REPLICAS = 4


def block_scale(key, dims, split, low, top_value):
    factor_of, own = 1.0, jax.random.fold_in(key, 6)
    for axis_at, shards_of in split:
        steps = jnp.exp(jax.random.uniform(jax.random.fold_in(own, axis_at), (shards_of,), jnp.float32, low / len(split), top_value / len(split)))
        factor_of = factor_of * jnp.repeat(steps, dims[axis_at] // shards_of).reshape([-1 if axis == axis_at else 1 for axis in range(len(dims))])
    return factor_of


def scatter_about(own_key, extent, spread, bound, pieces=(), dtype=jnp.bfloat16):
    level = block_scale(own_key, extent, pieces, -0.22, 0.18) if pieces else 1.0
    array = jax.random.normal(own_key, extent, jnp.float32) * spread * level
    return jnp.minimum(jnp.maximum(array, -bound), bound).astype(dtype)


def setup_inputs(seed: int = 0) -> dict:
    splits = jax.random.split(jax.random.key(seed), 3)
    return {
        "accumulated": scatter_about(splits[0], (REPLICAS, HID, D), 1.0, 6.0, ((0, 4), (1, 8))),
        "start_q": scatter_about(splits[1], (D, R), 1.0, 6.0, (), jnp.float32),
    }


def reference(accumulated, start_q):
    q_bf = start_q.astype(jnp.bfloat16)

    def left_factor(block):
        return jnp.dot(block.astype(jnp.float32), q_bf.astype(jnp.float32), preferred_element_type=jnp.float32)
    summed_p = jnp.sum(lax.map(left_factor, accumulated), axis=0) / REPLICAS
    gram = jnp.dot(summed_p.T, summed_p, precision=lax.Precision.HIGHEST)
    chol_lower = jnp.linalg.cholesky(gram)
    ortho = lax.linalg.triangular_solve(chol_lower, summed_p, left_side=False, lower=True, transpose_a=True)
    ortho_bf = ortho.astype(jnp.bfloat16)

    def right_factor(block):
        return lax.dot_general(block.astype(jnp.float32), ortho_bf.astype(jnp.float32), (((0,), (0,)), ((), ())), preferred_element_type=jnp.float32)
    new_q = jnp.sum(lax.map(right_factor, accumulated), axis=0) / REPLICAS
    update = lax.dot_general(ortho_bf.astype(jnp.float32), new_q.astype(jnp.bfloat16).astype(jnp.float32), (((1,), (1,)), ((), ())), preferred_element_type=jnp.float32)
    new_error = (accumulated.astype(jnp.float32) - update[None]).astype(jnp.bfloat16)
    return (update, new_error)
```

```python
import functools

import jax
import jax.numpy as jnp
from jax import lax
from jax.experimental import pallas as pl
from jax.experimental.pallas import tpu as pltpu
from jax.sharding import PartitionSpec as P

MESH = pl.DeviceIdType.MESH
HIGHEST = lax.Precision.HIGHEST
GROUPS = 4
BLOCK = 256
LAG = 4
AHEAD = 4
EARLY = 2
UNROLL = 4
VMEM_BYTES = 30 * 1024 * 1024


def chunks_of(rows):
    for count in (7, 8, 14, 4, 2):
        if rows % (128 * count) == 0:
            return count
    return 1


def copy_to(axis, target, src, dst, send_sem, recv_sem):
    return pltpu.make_async_remote_copy(
        src_ref=src, dst_ref=dst, send_sem=send_sem, recv_sem=recv_sem,
        device_id={axis: target}, device_id_type=MESH,
    )


def greet_line(barrier, n, d):
    @pl.when(d > 0)
    def _():
        pl.semaphore_signal(barrier, inc=1, device_id={"dp": d - 1}, device_id_type=MESH)

    @pl.when(d < n - 1)
    def _():
        pl.semaphore_signal(barrier, inc=1, device_id={"dp": d + 1}, device_id_type=MESH)


def line_of(n, d):
    half = n // 2
    left = d < half
    inner = jnp.where(left, d + 1, d - 1)
    outer = jnp.where(left, d - 1, d + 1)
    edge = (d == 0) | (d == n - 1)
    mid = (d == half - 1) | (d == half)
    return inner, outer, edge, mid


def factors_kernel(n, bits, count, a_hbm, q_hbm, a_v, ortho_ref, nq_ref, q_v, tot, own, part, cross, z, got,
                   full, gwork, ghalf, ggot, m_ref, zpart, zcross, q_sem, a_sem, in_send, out_send, part_recv,
                   cross_recv, tot_recv, rs_send, rs_recv, ag_send, ag_recv, g_send, g_recv, zin_send, zout_send,
                   zpart_recv, zcross_recv, ztot_recv):
    rows, wide = a_hbm.shape
    rank = q_hbm.shape[1]
    rg = rank // GROUPS
    rb = rows // count
    blocks = wide // 128
    total = GROUPS * count
    d = lax.axis_index("dp")
    me = lax.axis_index("mp")
    inner, outer, edge, mid = line_of(n, d)

    def bit(b):
        return lax.rem(me // (1 << b), 2)

    def partner(b):
        return me + (1 - 2 * bit(b)) * (1 << b)

    def some_rows(c):
        return pl.ds(pl.multiple_of(c * rb, rb), rb)

    def load(c):
        return pltpu.make_async_copy(a_hbm.at[some_rows(c)], a_v.at[some_rows(c)], a_sem.at[c])

    def piece(ref, g, c):
        return ref.at[c, pl.ds(pl.multiple_of(g * rg, rg), rg)]

    def send_part(g, c):
        return copy_to("dp", inner, piece(own, g, c), piece(part, g, c), in_send.at[g, c], part_recv.at[g, c])

    def send_cross(g, c):
        return copy_to("dp", inner, piece(own, g, c), piece(cross, g, c), in_send.at[g, c], cross_recv.at[g, c])

    def send_tot(g, c):
        return copy_to("dp", outer, piece(tot, g, c), piece(tot, g, c), out_send.at[g, c], tot_recv.at[g, c])

    def inward(crossing, passing):
        @pl.when(mid)
        def _():
            crossing.start()

        @pl.when(jnp.logical_not(mid))
        def _():
            passing.start()

    load_q = pltpu.make_async_copy(q_hbm, q_v, q_sem)
    load_q.start()
    load(0).start()
    barrier = pltpu.get_barrier_semaphore()
    greet_line(barrier, n, d)
    for b in range(bits):
        pl.semaphore_signal(barrier, inc=1, device_id={"mp": partner(b)}, device_id_type=MESH)
    gwork[...] = jnp.zeros_like(gwork)
    z[...] = jnp.zeros_like(z)
    load_q.wait()
    for c in range(1, count):
        load(c).start()
    q_bf = q_v[...].astype(jnp.bfloat16)

    def front(t):
        g, c = t // count, lax.rem(t, count)

        @pl.when(jnp.logical_not(edge))
        def _():
            send_part(g, c).wait_recv()
            mine = piece(own, g, c)
            mine[...] = mine[...] + piece(part, g, c)[...]
            inward(send_cross(g, c), send_part(g, c))

    early = min(EARLY, count)
    ahead = max(AHEAD, count - LAG)
    for c in range(count):
        load(c).wait()
        own[c] = jnp.dot(a_v[c * rb:(c + 1) * rb, :], q_bf, preferred_element_type=jnp.float32).T
        if c == early - 1:
            pl.semaphore_wait(barrier, jnp.where(d > 0, 1, 0) + jnp.where(d < n - 1, 1, 0) + bits)
        if c >= early - 1:
            @pl.when(edge)
            def _():
                for k in range(0 if c == early - 1 else c, c + 1):
                    inward(send_cross(0, k), send_part(0, k))
        if c >= ahead:
            front(c - ahead)

    @pl.when(edge)
    def _():
        def rest(t, carry):
            g, c = t // count, lax.rem(t, count)
            inward(send_cross(g, c), send_part(g, c))
            return carry

        lax.fori_loop(count, total, rest, 0)

    def exchange(t, carry):
        @pl.when(t < total)
        def _():
            front(t)

        @pl.when(t >= LAG)
        def _():
            g, c = (t - LAG) // count, lax.rem(t - LAG, count)

            @pl.when(mid)
            def _():
                send_cross(g, c).wait_recv()
                piece(tot, g, c)[...] = piece(own, g, c)[...] + piece(cross, g, c)[...]

            @pl.when(jnp.logical_not(mid))
            def _():
                send_tot(g, c).wait_recv()

            @pl.when(jnp.logical_not(edge))
            def _():
                send_tot(g, c).start()

            mean = piece(tot, g, c)[...] / n
            high = mean.astype(jnp.bfloat16)
            low = (mean - high.astype(jnp.float32)).astype(jnp.bfloat16)
            both = jnp.concatenate([high, low], axis=0)
            step = 512 if wide % 512 == 0 else 128
            for col in range(0, wide, step):
                sums = jnp.dot(both, a_v[some_rows(c), col:col + step], preferred_element_type=jnp.float32)
                for k in range(step // 128):
                    at, cols = (col // 128 + k) * rg, slice(k * 128, k * 128 + 128)
                    z[g, at:at + rg, :] += sums[:rg, cols] + sums[rg:, cols]

            @pl.when(g == GROUPS - 1)
            def _():
                whole = tot[c] / n
                gwork[...] += lax.dot_general(
                    whole, whole, (((1,), (1,)), ((), ())), precision=HIGHEST,
                    preferred_element_type=jnp.float32,
                )

        return carry

    orders = (tuple(range(bits)), (0,) + tuple(range(bits - 1, 0, -1)))
    lengths = [blocks * rg // 2 >> j for j in range(bits + 1)]
    offs = []
    for s in range(2):
        at = [s * lengths[0]]
        for j in range(bits):
            at.append(pl.multiple_of(at[j] + bit(orders[s][j]) * lengths[j + 1], lengths[bits]))
        offs.append(at)

    def rs(g, s, j):
        half = lengths[j + 1]
        b = orders[s][j]
        away = pl.multiple_of(offs[s][j] + (1 - bit(b)) * half, lengths[bits])
        spot = lengths[0] - lengths[j]
        return copy_to(
            "mp", partner(b), z.at[g, pl.ds(away, half)], got.at[g, s, spot:spot + half],
            rs_send.at[g, s, j], rs_recv.at[g, s, j],
        )

    def reduce_step(g, j):
        for s in range(2):
            if j > 0:
                half, spot = lengths[j], lengths[0] - lengths[j - 1]
                rs(g, s, j - 1).wait()
                keep = pl.ds(offs[s][j], half)
                z[g, keep, :] = z[g, keep, :] + got[g, s, spot:spot + half, :]
            if j < bits:
                rs(g, s, j).start()

    top = rank // 2
    mine_half = pl.ds(pl.multiple_of(bit(0) * top, top), top)
    other_half = pl.ds(pl.multiple_of((1 - bit(0)) * top, top), top)

    def gram(j):
        if j == 0:
            src, dst, b = gwork.at[other_half], ggot.at[0], 0
        elif j < bits:
            src, dst, b = ghalf.at[j - 1], ggot.at[j], j
        else:
            src, dst, b = m_ref.at[mine_half], m_ref.at[mine_half], 0
        return copy_to("mp", partner(b), src, dst, g_send.at[j], g_recv.at[j])

    def gram_step(j):
        if j > 0:
            gram(j - 1).wait()
        if 0 < j <= bits:
            before = gwork[mine_half, :] if j == 1 else ghalf[j - 2]
            if j < bits:
                ghalf[j - 1] = before + ggot[j - 1]
            else:
                m_ref[mine_half, :] = before + ggot[j - 1]
        if j <= bits:
            gram(j).start()

    def share(ref, g, s):
        return ref.at[g, pl.ds(offs[s][bits], lengths[bits])]

    def z_part(g, s):
        return copy_to("dp", inner, share(z, g, s), zpart.at[g, s], zin_send.at[g, s], zpart_recv.at[g, s])

    def z_cross(g, s):
        return copy_to("dp", inner, share(z, g, s), zcross.at[g, s], zin_send.at[g, s], zcross_recv.at[g, s])

    def z_tot(g, s):
        return copy_to("dp", outer, share(full, g, s), share(full, g, s), zout_send.at[g, s], ztot_recv.at[g, s])

    def line_edge(g):
        @pl.when(edge)
        def _():
            for s in range(2):
                inward(z_cross(g, s), z_part(g, s))

    def line_in(g):
        @pl.when(jnp.logical_not(edge))
        def _():
            for s in range(2):
                z_part(g, s).wait_recv()
                mine = share(z, g, s)
                mine[...] = mine[...] + zpart[g, s]
                inward(z_cross(g, s), z_part(g, s))

    def line_out(g):
        for s in range(2):
            @pl.when(mid)
            def _():
                z_cross(g, s).wait_recv()
                share(full, g, s)[...] = share(z, g, s)[...] + zcross[g, s]

            @pl.when(jnp.logical_not(mid))
            def _():
                z_tot(g, s).wait_recv()

            @pl.when(jnp.logical_not(edge))
            def _():
                z_tot(g, s).start()

    def ag(g, s, j):
        mine = full.at[g, pl.ds(offs[s][j + 1], lengths[j + 1])]
        return copy_to("mp", partner(orders[s][j]), mine, mine, ag_send.at[g, s, j], ag_recv.at[g, s, j])

    def gather_step(g, k):
        for s in range(2):
            if k > 0:
                ag(g, s, bits - k).wait()
            if k < bits:
                ag(g, s, bits - 1 - k).start()

    def inverse():
        m = m_ref[...]
        row = lax.broadcasted_iota(jnp.int32, (rank, rank), 0)
        lane = lax.broadcasted_iota(jnp.int32, (rank, rank), 1)
        pivots = jnp.sum(jnp.where(row == lane, m, 0.0), axis=1, keepdims=True)
        return jnp.where(lane < row, m, jnp.where(lane == row, 1.0, 0.0)) / jnp.sqrt(pivots)

    def straighten():
        w = inverse()

        def rows_of(c, carry):
            ortho_ref[some_rows(c), :] = jnp.dot(
                w, tot[c] / n, precision=HIGHEST, preferred_element_type=jnp.float32
            ).T.astype(jnp.bfloat16)
            return carry

        lax.fori_loop(0, count, rows_of, 0)

    def work(name, g, j):
        if name == "reduce":
            reduce_step(g, j)
        elif name == "edge":
            line_edge(g)
        elif name == "in":
            line_in(g)
        elif name == "out":
            line_out(g)
        elif name == "gather":
            gather_step(g, j)
        elif name == "gram":
            gram_step(j)
        elif name == "eliminate":
            eliminate(m_ref, rank * j // 4, rank * (j + 1) // 4)
        elif name == "straighten":
            straighten()

    at = max(count - ahead, 0)
    for when, entry in timetable(bits, count):
        if when > at:
            lax.fori_loop(at, when, exchange, 0)
            at = when
        work(*entry)

    w = inverse()
    together = 8 if blocks % 8 == 0 else 1

    def turn(first, carry):
        for k in range(together):
            block = first * together + k
            rows_of = pl.ds(pl.multiple_of(block * rg, rg), rg)
            right = jnp.concatenate([full[g, rows_of, :] for g in range(GROUPS)], axis=0)
            nq_ref[:, pl.ds(pl.multiple_of(block * 128, 128), 128)] = (
                jnp.dot(w, right, precision=HIGHEST, preferred_element_type=jnp.float32) / n
            ).astype(jnp.bfloat16)
        return carry

    lax.fori_loop(0, blocks // together, turn, 0)

    def sent(t, carry):
        g, c = t // count, lax.rem(t, count)
        send_part(g, c).wait_send()

        @pl.when(jnp.logical_not(edge))
        def _():
            send_tot(g, c).wait_send()

        return carry

    lax.fori_loop(0, total, sent, 0)
    for g in range(GROUPS):
        for s in range(2):
            z_part(g, s).wait_send()

        @pl.when(jnp.logical_not(edge))
        def _():
            for s in range(2):
                z_tot(g, s).wait_send()


def timetable(bits, count):
    end = GROUPS * count + LAG
    table = []
    for g in range(GROUPS - 1):
        done = (g + 1) * count + LAG
        delays = [0, 2] + [2 + -(-9 * j // (bits - 1)) for j in range(1, bits)]
        table += [(done + delay, ("reduce", g, j)) for j, delay in enumerate(delays)]
        table.append((done + delays[bits] + 2, ("edge", g, 0)))
    tail = [entry for when, entry in table if when >= end]
    table = sorted((pair for pair in table if pair[0] < end), key=lambda pair: pair[0])
    ordered = [("reduce", 3, 0), ("gram", 0, 0)]
    ordered += [entry for entry in tail if entry[1] < 2]
    late = [entry for entry in tail if entry[1] == 2]
    ordered += late[:1] + [("in", 0, 0), ("reduce", 3, 1), ("gram", 0, 1)] + late[1:]
    ordered += [("out", 0, 0), ("gather", 0, 0), ("in", 1, 0), ("gram", 0, 2)]
    ordered += [("reduce", 3, j) for j in range(2, bits)]
    ordered += [("gather", 0, 1)]
    ordered += [("gram", 0, j) for j in range(3, bits + 1)]
    ordered += [("reduce", 3, bits), ("edge", 3, 0), ("out", 1, 0), ("gather", 1, 0), ("in", 2, 0)]
    ordered += [("gram", 0, bits + 1), ("eliminate", 0, 0)]
    ordered += [("gather", 0, j) for j in range(2, bits)]
    ordered += [("gather", 1, 1), ("eliminate", 0, 1), ("out", 2, 0), ("gather", 2, 0), ("in", 3, 0)]
    ordered += [("gather", 0, bits)]
    ordered += [("gather", 1, j) for j in range(2, bits)]
    ordered += [("eliminate", 0, 2), ("gather", 2, 1), ("gather", 1, bits), ("eliminate", 0, 3)]
    ordered += [("gather", 2, j) for j in range(2, bits)]
    ordered += [("straighten", 0, 0), ("out", 3, 0), ("gather", 3, 0), ("gather", 2, bits)]
    ordered += [("gather", 3, j) for j in range(1, bits + 1)]
    return table + [(end, entry) for entry in ordered]


def eliminate(m_ref, first, last):
    size = m_ref.shape[1]
    top = first // 8 * 8
    row = top + lax.broadcasted_iota(jnp.int32, (size - top, size), 0)
    lane = lax.broadcasted_iota(jnp.int32, (size - top, size), 1)
    lane1 = lax.broadcasted_iota(jnp.int32, (1, size), 1)

    def pivots(t, carry):
        k = t * UNROLL
        m = m_ref[top:, :]
        lines = [m_ref[pl.ds(k + i, 1), :] for i in range(UNROLL)]
        cols = [jnp.sum(jnp.where(lane == k + j, m, 0.0), axis=1, keepdims=True) for j in range(UNROLL)]
        corner = {
            (i, j): jnp.sum(jnp.where(lane1 == k + j, lines[i], 0.0), axis=1, keepdims=True)
            for i in range(UNROLL) for j in range(i + 1)
        }
        out = jnp.where((lane >= k) & (lane < k + UNROLL), 0.0, m)
        for j in range(UNROLL):
            scale = 1.0 / corner[j, j]
            line = jnp.where(lane1 == k + j, 1.0, lines[j])
            for i in range(j + 1, UNROLL):
                factor = corner[i, j] * scale
                lines[i] = jnp.where(lane1 == k + j, 0.0, lines[i]) - factor * line
                for l in range(j + 1, i + 1):
                    corner[i, l] = corner[i, l] - factor * corner[l, j]
            factor = cols[j] * scale
            for l in range(j + 1, UNROLL):
                cols[l] = cols[l] - factor * corner[l, j]
            out = out - factor * jnp.where((lane1 > k + j) & (lane1 < k + UNROLL), 0.0, line)
        m_ref[top:, :] = jnp.where(row >= k + UNROLL, out, m)
        for i in range(1, UNROLL):
            m_ref[pl.ds(k + i, 1), :] = lines[i]
        return carry

    lax.fori_loop(first // UNROLL, last // UNROLL, pivots, 0)


def last_kernel(a_ref, ortho_ref, nq_ref, update_ref, error_ref):
    small, wide = update_ref.shape
    some = pl.ds(pl.multiple_of(pl.program_id(0) * small, small), small)
    ortho = ortho_ref[some, :]
    group = 512 if wide % 512 == 0 else 128
    for first in range(0, wide, group):
        cols = slice(first, first + group)
        update = jnp.dot(ortho, nq_ref[:, cols], preferred_element_type=jnp.float32)
        update_ref[:, cols] = update
        error_ref[:, cols] = (a_ref[some, cols].astype(jnp.float32) - update).astype(jnp.bfloat16)


def on_device(accumulated, start_q):
    a = accumulated[0]
    rows, wide = a.shape
    rank = start_q.shape[1]
    n, peers = lax.axis_size("dp"), lax.axis_size("mp")
    bits = peers.bit_length() - 1
    assert peers == 1 << bits and bits >= 2 and n >= 2 and rank == 128
    count = chunks_of(rows)
    rb = rows // count
    f32, bf16 = jnp.float32, jnp.bfloat16
    vmem = pl.BlockSpec(memory_space=pltpu.VMEM)
    hbm = pl.BlockSpec(memory_space=pltpu.HBM)
    dma = pltpu.SemaphoreType.DMA
    flat = wide // GROUPS
    a_v, ortho, new_q = pl.pallas_call(
        functools.partial(factors_kernel, n, bits, count),
        out_shape=(pltpu.VMEM((rows, wide), bf16), pltpu.VMEM((rows, rank), bf16), pltpu.VMEM((rank, wide), bf16)),
        in_specs=[hbm, hbm],
        out_specs=(vmem, vmem, vmem),
        scratch_shapes=[
            pltpu.VMEM((wide, rank), f32),
            pltpu.VMEM((count, rank, rb), f32),
            pltpu.VMEM((count, rank, rb), f32),
            pltpu.VMEM((count, rank, rb), f32),
            pltpu.VMEM((count, rank, rb), f32),
            pltpu.VMEM((GROUPS, flat, 128), f32),
            pltpu.VMEM((GROUPS, 2, flat // 2, 128), f32),
            pltpu.VMEM((GROUPS, flat, 128), f32),
            pltpu.VMEM((rank, rank), f32),
            pltpu.VMEM((bits - 1, rank // 2, rank), f32),
            pltpu.VMEM((bits, rank // 2, rank), f32),
            pltpu.VMEM((rank, rank), f32),
            pltpu.VMEM((GROUPS, 2, flat // 2 // peers, 128), f32),
            pltpu.VMEM((GROUPS, 2, flat // 2 // peers, 128), f32),
            dma,
            dma((count,)),
        ] + [dma((GROUPS, count))] * 5 + [dma((GROUPS, 2, bits))] * 4 + [dma((bits + 1,))] * 2
        + [dma((GROUPS, 2))] * 5,
        compiler_params=pltpu.CompilerParams(
            collective_id=0, has_side_effects=True, vmem_limit_bytes=VMEM_BYTES
        ),
        name="factors",
    )(a, pltpu.with_memory_space_constraint(start_q, pltpu.HBM))
    small = BLOCK if rows % BLOCK == 0 else rb
    update, error = pl.pallas_call(
        last_kernel,
        grid=(rows // small,),
        out_shape=(
            jax.ShapeDtypeStruct((rows, wide), f32),
            jax.ShapeDtypeStruct((rows, wide), bf16),
        ),
        in_specs=[vmem, vmem, vmem],
        out_specs=(
            pl.BlockSpec((small, wide), lambda i: (i, 0)),
            pl.BlockSpec((small, wide), lambda i: (i, 0)),
        ),
        compiler_params=pltpu.CompilerParams(vmem_limit_bytes=VMEM_BYTES),
        name="decompress",
    )(a_v, ortho, new_q)
    return (update, error[None])


def solution(mesh):
    placed = (P("dp", "mp", None), P())
    return jax.shard_map(
        on_device,
        mesh=mesh,
        in_specs=placed,
        out_specs=(P("mp", None), P("dp", "mp", None)),
        check_vma=False,
    )
```

```python
import functools

import jax
import jax.numpy as jnp
from jax import lax
from jax.experimental import pallas as pl
from jax.experimental.pallas import tpu as pltpu
from jax.sharding import PartitionSpec as P

MESH = pl.DeviceIdType.MESH
HIGHEST = lax.Precision.HIGHEST
GROUPS = 4
STRIP = 1024
SLOTS = 4
LAG = 4
AHEAD = 4
EARLY = 2
UNROLL = 4
VMEM_BYTES = 30 * 1024 * 1024


def chunks_of(rows):
    for count in (7, 8, 14, 4, 2):
        if rows % (128 * count) == 0:
            return count
    return 1


def copy_to(axis, target, src, dst, send_sem, recv_sem):
    return pltpu.make_async_remote_copy(
        src_ref=src, dst_ref=dst, send_sem=send_sem, recv_sem=recv_sem,
        device_id={axis: target}, device_id_type=MESH,
    )


def greet_line(barrier, n, d):
    @pl.when(d > 0)
    def _():
        pl.semaphore_signal(barrier, inc=1, device_id={"dp": d - 1}, device_id_type=MESH)

    @pl.when(d < n - 1)
    def _():
        pl.semaphore_signal(barrier, inc=1, device_id={"dp": d + 1}, device_id_type=MESH)


def line_of(n, d):
    half = n // 2
    left = d < half
    inner = jnp.where(left, d + 1, d - 1)
    outer = jnp.where(left, d - 1, d + 1)
    edge = (d == 0) | (d == n - 1)
    mid = (d == half - 1) | (d == half)
    return inner, outer, edge, mid


def factors_kernel(n, bits, count, a_hbm, q_hbm, a_v, tot, full, m_ref, q_v, own, part, cross, z, got,
                   gwork, ghalf, ggot, zpart, zcross, q_sem, a_sem, in_send, out_send, part_recv,
                   cross_recv, tot_recv, rs_send, rs_recv, ag_send, ag_recv, g_send, g_recv, zin_send, zout_send,
                   zpart_recv, zcross_recv, ztot_recv):
    rows, wide = a_hbm.shape
    rank = q_hbm.shape[1]
    rg = rank // GROUPS
    rb = rows // count
    blocks = wide // 128
    total = GROUPS * count
    d = lax.axis_index("dp")
    me = lax.axis_index("mp")
    inner, outer, edge, mid = line_of(n, d)

    def bit(b):
        return lax.rem(me // (1 << b), 2)

    def partner(b):
        return me + (1 - 2 * bit(b)) * (1 << b)

    def some_rows(c):
        return pl.ds(pl.multiple_of(c * rb, rb), rb)

    def load(c):
        return pltpu.make_async_copy(a_hbm.at[some_rows(c)], a_v.at[some_rows(c)], a_sem.at[c])

    def piece(ref, g, c):
        return ref.at[c, pl.ds(pl.multiple_of(g * rg, rg), rg)]

    def send_part(g, c):
        return copy_to("dp", inner, piece(own, g, c), piece(part, g, c), in_send.at[g, c], part_recv.at[g, c])

    def send_cross(g, c):
        return copy_to("dp", inner, piece(own, g, c), piece(cross, g, c), in_send.at[g, c], cross_recv.at[g, c])

    def send_tot(g, c):
        return copy_to("dp", outer, piece(tot, g, c), piece(tot, g, c), out_send.at[g, c], tot_recv.at[g, c])

    def inward(crossing, passing):
        @pl.when(mid)
        def _():
            crossing.start()

        @pl.when(jnp.logical_not(mid))
        def _():
            passing.start()

    load_q = pltpu.make_async_copy(q_hbm, q_v, q_sem)
    load_q.start()
    load(0).start()
    barrier = pltpu.get_barrier_semaphore()
    greet_line(barrier, n, d)
    for b in range(bits):
        pl.semaphore_signal(barrier, inc=1, device_id={"mp": partner(b)}, device_id_type=MESH)
    gwork[...] = jnp.zeros_like(gwork)
    z[...] = jnp.zeros_like(z)
    load_q.wait()
    for c in range(1, count):
        load(c).start()
    q_bf = q_v[...].astype(jnp.bfloat16)

    def front(t):
        g, c = t // count, lax.rem(t, count)

        @pl.when(jnp.logical_not(edge))
        def _():
            send_part(g, c).wait_recv()
            mine = piece(own, g, c)
            mine[...] = mine[...] + piece(part, g, c)[...]
            inward(send_cross(g, c), send_part(g, c))

    early = min(EARLY, count)
    ahead = max(AHEAD, count - LAG)
    for c in range(count):
        load(c).wait()
        own[c] = jnp.dot(a_v[c * rb:(c + 1) * rb, :], q_bf, preferred_element_type=jnp.float32).T
        if c == early - 1:
            pl.semaphore_wait(barrier, jnp.where(d > 0, 1, 0) + jnp.where(d < n - 1, 1, 0) + bits)
        if c >= early - 1:
            @pl.when(edge)
            def _():
                for k in range(0 if c == early - 1 else c, c + 1):
                    inward(send_cross(0, k), send_part(0, k))
        if c >= ahead:
            front(c - ahead)

    @pl.when(edge)
    def _():
        def rest(t, carry):
            g, c = t // count, lax.rem(t, count)
            inward(send_cross(g, c), send_part(g, c))
            return carry

        lax.fori_loop(count, total, rest, 0)

    def exchange(t, carry):
        @pl.when(t < total)
        def _():
            front(t)

        @pl.when(t >= LAG)
        def _():
            g, c = (t - LAG) // count, lax.rem(t - LAG, count)

            @pl.when(mid)
            def _():
                send_cross(g, c).wait_recv()
                piece(tot, g, c)[...] = piece(own, g, c)[...] + piece(cross, g, c)[...]

            @pl.when(jnp.logical_not(mid))
            def _():
                send_tot(g, c).wait_recv()

            @pl.when(jnp.logical_not(edge))
            def _():
                send_tot(g, c).start()

            mean = piece(tot, g, c)[...] / n
            high = mean.astype(jnp.bfloat16)
            low = (mean - high.astype(jnp.float32)).astype(jnp.bfloat16)
            both = jnp.concatenate([high, low], axis=0)
            step = 512 if wide % 512 == 0 else 128
            for col in range(0, wide, step):
                sums = jnp.dot(both, a_v[some_rows(c), col:col + step], preferred_element_type=jnp.float32)
                for k in range(step // 128):
                    at, cols = (col // 128 + k) * rg, slice(k * 128, k * 128 + 128)
                    z[g, at:at + rg, :] += sums[:rg, cols] + sums[rg:, cols]

            @pl.when(g == GROUPS - 1)
            def _():
                whole = tot[c] / n
                gwork[...] += lax.dot_general(
                    whole, whole, (((1,), (1,)), ((), ())), precision=HIGHEST,
                    preferred_element_type=jnp.float32,
                )

        return carry

    orders = (tuple(range(bits)), (0,) + tuple(range(bits - 1, 0, -1)))
    lengths = [blocks * rg // 2 >> j for j in range(bits + 1)]
    offs = []
    for s in range(2):
        at = [s * lengths[0]]
        for j in range(bits):
            at.append(pl.multiple_of(at[j] + bit(orders[s][j]) * lengths[j + 1], lengths[bits]))
        offs.append(at)

    def rs(g, s, j):
        half = lengths[j + 1]
        b = orders[s][j]
        away = pl.multiple_of(offs[s][j] + (1 - bit(b)) * half, lengths[bits])
        spot = lengths[0] - lengths[j]
        return copy_to(
            "mp", partner(b), z.at[g, pl.ds(away, half)], got.at[g, s, spot:spot + half],
            rs_send.at[g, s, j], rs_recv.at[g, s, j],
        )

    def reduce_step(g, j, pass_on=False):
        for s in range(2):
            if j > 0:
                half, spot = lengths[j], lengths[0] - lengths[j - 1]
                rs(g, s, j - 1).wait()
                keep = pl.ds(offs[s][j], half)
                z[g, keep, :] = z[g, keep, :] + got[g, s, spot:spot + half, :]
            if j < bits:
                rs(g, s, j).start()
            if pass_on:
                line_edge(g, s)

    top = rank // 2
    mine_half = pl.ds(pl.multiple_of(bit(0) * top, top), top)
    other_half = pl.ds(pl.multiple_of((1 - bit(0)) * top, top), top)

    def gram(j):
        if j == 0:
            src, dst, b = gwork.at[other_half], ggot.at[0], 0
        elif j < bits:
            src, dst, b = ghalf.at[j - 1], ggot.at[j], j
        else:
            src, dst, b = m_ref.at[mine_half], m_ref.at[mine_half], 0
        return copy_to("mp", partner(b), src, dst, g_send.at[j], g_recv.at[j])

    def gram_step(j):
        if j > 0:
            gram(j - 1).wait()
        if 0 < j <= bits:
            before = gwork[mine_half, :] if j == 1 else ghalf[j - 2]
            if j < bits:
                ghalf[j - 1] = before + ggot[j - 1]
            else:
                m_ref[mine_half, :] = before + ggot[j - 1]
        if j <= bits:
            gram(j).start()

    def share(ref, g, s):
        return ref.at[g, pl.ds(offs[s][bits], lengths[bits])]

    def z_part(g, s):
        return copy_to("dp", inner, share(z, g, s), zpart.at[g, s], zin_send.at[g, s], zpart_recv.at[g, s])

    def z_cross(g, s):
        return copy_to("dp", inner, share(z, g, s), zcross.at[g, s], zin_send.at[g, s], zcross_recv.at[g, s])

    def z_tot(g, s):
        return copy_to("dp", outer, share(full, g, s), share(full, g, s), zout_send.at[g, s], ztot_recv.at[g, s])

    def line_edge(g, s):
        @pl.when(edge)
        def _():
            inward(z_cross(g, s), z_part(g, s))

    def line_in(g):
        @pl.when(jnp.logical_not(edge))
        def _():
            for s in range(2):
                z_part(g, s).wait_recv()
                mine = share(z, g, s)
                mine[...] = mine[...] + zpart[g, s]
                inward(z_cross(g, s), z_part(g, s))

    def line_out(g, gather):
        for s in range(2):
            @pl.when(mid)
            def _():
                z_cross(g, s).wait_recv()
                share(full, g, s)[...] = share(z, g, s)[...] + zcross[g, s]

            @pl.when(jnp.logical_not(mid))
            def _():
                z_tot(g, s).wait_recv()

            @pl.when(jnp.logical_not(edge))
            def _():
                z_tot(g, s).start()

            if gather:
                ag(g, s, bits - 1).start()

    def ag(g, s, j):
        mine = full.at[g, pl.ds(offs[s][j + 1], lengths[j + 1])]
        return copy_to("mp", partner(orders[s][j]), mine, mine, ag_send.at[g, s, j], ag_recv.at[g, s, j])

    def gather_step(g, k):
        for s in range(2):
            if k > 0:
                ag(g, s, bits - k).wait()
            if k < bits:
                ag(g, s, bits - 1 - k).start()

    def work(name, g, j):
        if name == "reduce":
            reduce_step(g, j)
        elif name == "pass":
            reduce_step(g, bits, True)
        elif name == "edge":
            for s in range(2):
                line_edge(g, s)
        elif name == "in":
            line_in(g)
        elif name == "out":
            line_out(g, j)
        elif name == "gather":
            gather_step(g, j)
        elif name == "gram":
            gram_step(j)
        elif name == "eliminate":
            eliminate(m_ref, rank * j // 4, rank * (j + 1) // 4)

    at = max(count - ahead, 0)
    for when, entry in timetable(bits, count):
        if when > at:
            lax.fori_loop(at, when, exchange, 0)
            at = when
        work(*entry)

    def sent(t, carry):
        g, c = t // count, lax.rem(t, count)
        send_part(g, c).wait_send()

        @pl.when(jnp.logical_not(edge))
        def _():
            send_tot(g, c).wait_send()

        return carry

    lax.fori_loop(0, total, sent, 0)
    for g in range(GROUPS):
        for s in range(2):
            z_part(g, s).wait_send()

        @pl.when(jnp.logical_not(edge))
        def _():
            for s in range(2):
                z_tot(g, s).wait_send()


def timetable(bits, count):
    end = GROUPS * count + LAG
    table = []
    for g in range(GROUPS - 1):
        done = (g + 1) * count + LAG
        delays = [0, 2] + [2 + -(-9 * j // (bits - 1)) for j in range(1, bits)]
        table += [(done + delay, ("reduce", g, j)) for j, delay in enumerate(delays)]
        if g < 2:
            table.append((done + delays[bits] + 2, ("edge", g, 0)))
    tail = [entry for when, entry in table if when >= end and entry[1] < 2]
    table = sorted((pair for pair in table if pair[0] < end), key=lambda pair: pair[0])
    begun = sum(entry[:2] == ("reduce", 2) for _, entry in table)
    late = [("reduce", 2, j) for j in range(begun, bits)] + [("pass", 2, 0)]
    ordered = tail + [("reduce", 3, 0), ("gram", 0, 0)] + late[:-1]
    ordered += [("in", 0, 0), ("reduce", 3, 1), ("gram", 0, 1), late[-1], ("out", 0, 0), ("in", 1, 0)]
    ordered += [("reduce", 3, j) for j in range(2, bits)] + [("gram", 0, 2), ("pass", 3, 0), ("gather", 0, 0)]
    ordered += [("gram", 0, j) for j in range(3, bits + 1)]
    ordered += [("out", 1, 1), ("in", 2, 0), ("gram", 0, bits + 1), ("eliminate", 0, 0), ("gather", 0, 1)]
    ordered += [("out", 2, 1), ("gather", 1, 1), ("eliminate", 0, 1), ("in", 3, 0)]
    ordered += [("gather", 0, j) for j in range(2, bits)] + [("gather", 2, 1)]
    ordered += [("gather", 1, j) for j in range(2, bits)] + [("eliminate", 0, 2), ("gather", 0, bits)]
    ordered += [("gather", 2, j) for j in range(2, bits)] + [("out", 3, 1), ("gather", 1, bits)]
    ordered += [("eliminate", 0, 3), ("gather", 3, 1), ("gather", 2, bits)]
    ordered += [("gather", 3, j) for j in range(2, bits + 1)]
    return table + [(end, entry) for entry in ordered]


def eliminate(m_ref, first, last):
    size = m_ref.shape[1]
    top = first // 8 * 8
    row = top + lax.broadcasted_iota(jnp.int32, (size - top, size), 0)
    lane = lax.broadcasted_iota(jnp.int32, (size - top, size), 1)
    lane1 = lax.broadcasted_iota(jnp.int32, (1, size), 1)

    def pivots(t, carry):
        k = t * UNROLL
        m = m_ref[top:, :]
        lines = [m_ref[pl.ds(k + i, 1), :] for i in range(UNROLL)]
        cols = [jnp.sum(jnp.where(lane == k + j, m, 0.0), axis=1, keepdims=True) for j in range(UNROLL)]
        corner = {
            (i, j): jnp.sum(jnp.where(lane1 == k + j, lines[i], 0.0), axis=1, keepdims=True)
            for i in range(UNROLL) for j in range(i + 1)
        }
        out = jnp.where((lane >= k) & (lane < k + UNROLL), 0.0, m)
        for j in range(UNROLL):
            scale = 1.0 / corner[j, j]
            line = jnp.where(lane1 == k + j, 1.0, lines[j])
            for i in range(j + 1, UNROLL):
                factor = corner[i, j] * scale
                lines[i] = jnp.where(lane1 == k + j, 0.0, lines[i]) - factor * line
                for l in range(j + 1, i + 1):
                    corner[i, l] = corner[i, l] - factor * corner[l, j]
            factor = cols[j] * scale
            for l in range(j + 1, UNROLL):
                cols[l] = cols[l] - factor * corner[l, j]
            out = out - factor * jnp.where((lane1 > k + j) & (lane1 < k + UNROLL), 0.0, line)
        m_ref[top:, :] = jnp.where(row >= k + UNROLL, out, m)
        for i in range(1, UNROLL):
            m_ref[pl.ds(k + i, 1), :] = lines[i]
        return carry

    lax.fori_loop(first // UNROLL, last // UNROLL, pivots, 0)


def last_kernel(n, a_ref, tot, full, m_ref, update_hbm, error_hbm, ortho, nq, update, error, update_sem, error_sem):
    rows, wide = a_ref.shape
    count, rank, rb = tot.shape
    rg = rank // GROUPS
    slots, _, width = update.shape
    strips = wide // width
    m = m_ref[...]
    row = lax.broadcasted_iota(jnp.int32, (rank, rank), 0)
    lane = lax.broadcasted_iota(jnp.int32, (rank, rank), 1)
    pivots = jnp.sum(jnp.where(row == lane, m, 0.0), axis=1, keepdims=True)
    w = jnp.where(lane < row, m, jnp.where(lane == row, 1.0, 0.0)) / jnp.sqrt(pivots)

    def rows_of(r):
        return pl.ds(pl.multiple_of(r * rb, rb), rb)

    def cols_of(c):
        return pl.ds(pl.multiple_of(c * width, width), width)

    def straighten(r):
        ortho[rows_of(r), :] = jnp.dot(
            w, tot[r] / n, precision=HIGHEST, preferred_element_type=jnp.float32
        ).T.astype(jnp.bfloat16)

    def turn(c):
        for k in range(width // 128):
            some = pl.ds(pl.multiple_of((c * (width // 128) + k) * rg, rg), rg)
            right = jnp.concatenate([full[g, some, :] for g in range(GROUPS)], axis=0)
            nq[:, pl.ds(pl.multiple_of(c * width + k * 128, 128), 128)] = (
                jnp.dot(w, right, precision=HIGHEST, preferred_element_type=jnp.float32) / n
            ).astype(jnp.bfloat16)

    def write(slot, r, c):
        return (
            pltpu.make_async_copy(update.at[slot], update_hbm.at[rows_of(r), cols_of(c)], update_sem.at[slot]),
            pltpu.make_async_copy(error.at[slot], error_hbm.at[rows_of(r), cols_of(c)], error_sem.at[slot]),
        )

    def block(i, r, c):
        slot = lax.rem(i, slots)

        @pl.when(i >= slots)
        def _():
            for copy in write(slot, r, c):
                copy.wait()

        right = jnp.dot(ortho[rows_of(r), :], nq[:, cols_of(c)], preferred_element_type=jnp.float32)
        update[slot] = right
        error[slot] = (a_ref[rows_of(r), cols_of(c)].astype(jnp.float32) - right).astype(jnp.bfloat16)
        for copy in write(slot, r, c):
            copy.start()

    first = min(2, count)
    for r in range(first):
        straighten(r)

    def strip(c, carry):
        turn(c)
        for r in range(first):
            block(c * first + r, r, c)
        return carry

    lax.fori_loop(0, strips, strip, 0)

    def band(r, carry):
        straighten(r)

        def across(c, carry):
            block(r * strips + c, r, c)
            return carry

        return lax.fori_loop(0, strips, across, carry)

    lax.fori_loop(first, count, band, 0)
    for slot in range(min(slots, count * strips)):
        for copy in write(slot, 0, 0):
            copy.wait()


def on_device(accumulated, start_q):
    a = accumulated[0]
    rows, wide = a.shape
    rank = start_q.shape[1]
    n, peers = lax.axis_size("dp"), lax.axis_size("mp")
    bits = peers.bit_length() - 1
    assert peers == 1 << bits and bits >= 2 and n >= 2 and rank == 128
    count = chunks_of(rows)
    rb = rows // count
    f32, bf16 = jnp.float32, jnp.bfloat16
    vmem = pl.BlockSpec(memory_space=pltpu.VMEM)
    hbm = pl.BlockSpec(memory_space=pltpu.HBM)
    dma = pltpu.SemaphoreType.DMA
    flat = wide // GROUPS
    a_v, tot, full, lower = pl.pallas_call(
        functools.partial(factors_kernel, n, bits, count),
        out_shape=(
            pltpu.VMEM((rows, wide), bf16),
            pltpu.VMEM((count, rank, rb), f32),
            pltpu.VMEM((GROUPS, flat, 128), f32),
            pltpu.VMEM((rank, rank), f32),
        ),
        in_specs=[hbm, hbm],
        out_specs=(vmem,) * 4,
        scratch_shapes=[
            pltpu.VMEM((wide, rank), f32),
            pltpu.VMEM((count, rank, rb), f32),
            pltpu.VMEM((count, rank, rb), f32),
            pltpu.VMEM((count, rank, rb), f32),
            pltpu.VMEM((GROUPS, flat, 128), f32),
            pltpu.VMEM((GROUPS, 2, flat // 2, 128), f32),
            pltpu.VMEM((rank, rank), f32),
            pltpu.VMEM((bits - 1, rank // 2, rank), f32),
            pltpu.VMEM((bits, rank // 2, rank), f32),
            pltpu.VMEM((GROUPS, 2, flat // 2 // peers, 128), f32),
            pltpu.VMEM((GROUPS, 2, flat // 2 // peers, 128), f32),
            dma,
            dma((count,)),
        ] + [dma((GROUPS, count))] * 5 + [dma((GROUPS, 2, bits))] * 4 + [dma((bits + 1,))] * 2
        + [dma((GROUPS, 2))] * 5,
        compiler_params=pltpu.CompilerParams(
            collective_id=0, has_side_effects=True, vmem_limit_bytes=VMEM_BYTES
        ),
        name="factors",
    )(a, pltpu.with_memory_space_constraint(start_q, pltpu.HBM))
    width = STRIP if wide % STRIP == 0 else 128
    update, error = pl.pallas_call(
        functools.partial(last_kernel, n),
        out_shape=(
            jax.ShapeDtypeStruct((rows, wide), f32),
            jax.ShapeDtypeStruct((rows, wide), bf16),
        ),
        in_specs=[vmem] * 4,
        out_specs=(hbm, hbm),
        scratch_shapes=[
            pltpu.VMEM((rows, rank), bf16),
            pltpu.VMEM((rank, wide), bf16),
            pltpu.VMEM((SLOTS, rb, width), f32),
            pltpu.VMEM((SLOTS, rb, width), bf16),
            dma((SLOTS,)),
            dma((SLOTS,)),
        ],
        compiler_params=pltpu.CompilerParams(vmem_limit_bytes=VMEM_BYTES),
        name="decompress",
    )(a_v, tot, full, lower)
    return (update, error[None])


def solution(mesh):
    placed = (P("dp", "mp", None), P())
    return jax.shard_map(
        on_device,
        mesh=mesh,
        in_specs=placed,
        out_specs=(P("mp", None), P("dp", "mp", None)),
        check_vma=False,
    )
```

```python
import functools

import jax
import jax.numpy as jnp
from jax import lax
from jax.experimental import pallas as pl
from jax.experimental.pallas import tpu as pltpu
from jax.sharding import PartitionSpec as P

MESH = pl.DeviceIdType.MESH
HIGHEST = lax.Precision.HIGHEST
GROUPS = 4
SPANS = (9, 9, 9)
STRIP = 1024
SLOTS = 4
LAG = 4
AHEAD = 4
EARLY = 2
UNROLL = 4
VMEM_BYTES = 30 * 1024 * 1024


def chunks_of(rows):
    for count in (7, 8, 14, 4, 2):
        if rows % (128 * count) == 0:
            return count
    return 1


def copy_to(axis, target, src, dst, send_sem, recv_sem):
    return pltpu.make_async_remote_copy(
        src_ref=src, dst_ref=dst, send_sem=send_sem, recv_sem=recv_sem,
        device_id={axis: target}, device_id_type=MESH,
    )


def greet_line(barrier, n, d):
    @pl.when(d > 0)
    def _():
        pl.semaphore_signal(barrier, inc=1, device_id={"dp": d - 1}, device_id_type=MESH)

    @pl.when(d < n - 1)
    def _():
        pl.semaphore_signal(barrier, inc=1, device_id={"dp": d + 1}, device_id_type=MESH)


def line_of(n, d):
    half = n // 2
    left = d < half
    inner = jnp.where(left, d + 1, d - 1)
    outer = jnp.where(left, d - 1, d + 1)
    edge = (d == 0) | (d == n - 1)
    mid = (d == half - 1) | (d == half)
    return inner, outer, edge, mid


def factors_kernel(n, bits, count, sizes, a_hbm, q_hbm, a_v, tot, full, m_ref, q_v, own, part, cross, z, got,
                   gwork, ghalf, ggot, zpart, zcross, q_sem, a_sem, in_send, out_send, part_recv,
                   cross_recv, tot_recv, rs_send, rs_recv, ag_send, ag_recv, g_send, g_recv, zin_send, zout_send,
                   zpart_recv, zcross_recv, ztot_recv):
    rows, wide = a_hbm.shape
    rank = q_hbm.shape[1]
    firsts = [sum(sizes[:g]) for g in range(GROUPS)]
    rb = rows // count
    blocks = wide // 128
    total = GROUPS * count
    d = lax.axis_index("dp")
    me = lax.axis_index("mp")
    inner, outer, edge, mid = line_of(n, d)

    def bit(b):
        return lax.rem(me // (1 << b), 2)

    def partner(b):
        return me + (1 - 2 * bit(b)) * (1 << b)

    def some_rows(c):
        return pl.ds(pl.multiple_of(c * rb, rb), rb)

    def load(c):
        return pltpu.make_async_copy(a_hbm.at[some_rows(c)], a_v.at[some_rows(c)], a_sem.at[c])

    def piece(ref, g, c):
        return ref.at[c, pl.ds(firsts[g], sizes[g])]

    def send_part(g, c):
        return copy_to("dp", inner, piece(own, g, c), piece(part, g, c), in_send.at[g, c], part_recv.at[g, c])

    def send_cross(g, c):
        return copy_to("dp", inner, piece(own, g, c), piece(cross, g, c), in_send.at[g, c], cross_recv.at[g, c])

    def send_tot(g, c):
        return copy_to("dp", outer, piece(tot, g, c), piece(tot, g, c), out_send.at[g, c], tot_recv.at[g, c])

    def inward(crossing, passing):
        @pl.when(mid)
        def _():
            crossing.start()

        @pl.when(jnp.logical_not(mid))
        def _():
            passing.start()

    load_q = pltpu.make_async_copy(q_hbm, q_v, q_sem)
    load_q.start()
    load(0).start()
    barrier = pltpu.get_barrier_semaphore()
    greet_line(barrier, n, d)
    for b in range(bits):
        pl.semaphore_signal(barrier, inc=1, device_id={"mp": partner(b)}, device_id_type=MESH)
    gwork[...] = jnp.zeros_like(gwork)
    z[...] = jnp.zeros_like(z)
    load_q.wait()
    for c in range(1, count):
        load(c).start()
    q_bf = q_v[...].astype(jnp.bfloat16)

    def front(g, c):
        @pl.when(jnp.logical_not(edge))
        def _():
            send_part(g, c).wait_recv()
            mine = piece(own, g, c)
            mine[...] = mine[...] + piece(part, g, c)[...]
            inward(send_cross(g, c), send_part(g, c))

    early = min(EARLY, count)
    ahead = max(AHEAD, count - LAG)
    for c in range(count):
        load(c).wait()
        own[c] = jnp.dot(a_v[c * rb:(c + 1) * rb, :], q_bf, preferred_element_type=jnp.float32).T
        if c == early - 1:
            pl.semaphore_wait(barrier, jnp.where(d > 0, 1, 0) + jnp.where(d < n - 1, 1, 0) + bits)
        if c >= early - 1:
            @pl.when(edge)
            def _():
                for k in range(0 if c == early - 1 else c, c + 1):
                    inward(send_cross(0, k), send_part(0, k))
        if c >= ahead:
            front(0, c - ahead)

    @pl.when(edge)
    def _():
        for g in range(1, GROUPS):
            def rest(c, carry):
                inward(send_cross(g, c), send_part(g, c))
                return carry

            lax.fori_loop(0, count, rest, 0)

    def back(g, c):
        rg = sizes[g]

        @pl.when(mid)
        def _():
            send_cross(g, c).wait_recv()
            piece(tot, g, c)[...] = piece(own, g, c)[...] + piece(cross, g, c)[...]

        @pl.when(jnp.logical_not(mid))
        def _():
            send_tot(g, c).wait_recv()

        @pl.when(jnp.logical_not(edge))
        def _():
            send_tot(g, c).start()

        mean = piece(tot, g, c)[...] / n
        high = mean.astype(jnp.bfloat16)
        low = (mean - high.astype(jnp.float32)).astype(jnp.bfloat16)
        both = jnp.concatenate([high, low], axis=0)
        step = 512 if wide % 512 == 0 else 128
        for col in range(0, wide, step):
            sums = jnp.dot(both, a_v[some_rows(c), col:col + step], preferred_element_type=jnp.float32)
            for k in range(step // 128):
                at, cols = firsts[g] * blocks + (col // 128 + k) * rg, slice(k * 128, k * 128 + 128)
                z[at:at + rg, :] += sums[:rg, cols] + sums[rg:, cols]

        if g == GROUPS - 1:
            whole = tot[c] / n
            gwork[...] += lax.dot_general(
                whole, whole, (((1,), (1,)), ((), ())), precision=HIGHEST,
                preferred_element_type=jnp.float32,
            )

    def exchange(first, last):
        marks = [g * count + shift for g in range(GROUPS + 1) for shift in (0, LAG)]
        cuts = sorted({first, last} | {mark for mark in marks if first < mark < last})
        for low, high in zip(cuts, cuts[1:]):
            def step(t, carry):
                if low < total:
                    front(low // count, t - low // count * count)
                if low >= LAG:
                    g = (low - LAG) // count
                    back(g, t - LAG - g * count)
                return carry

            lax.fori_loop(low, high, step, 0)

    orders = (tuple(range(bits)), (0,) + tuple(range(bits - 1, 0, -1)))
    lengths = [[blocks * rg // 2 >> j for j in range(bits + 1)] for rg in sizes]
    offs = []
    for g in range(GROUPS):
        offs.append([])
        for s in range(2):
            at = [firsts[g] * blocks + s * lengths[g][0]]
            for j in range(bits):
                at.append(pl.multiple_of(at[j] + bit(orders[s][j]) * lengths[g][j + 1], 8))
            offs[g].append(at)

    def spot_of(g, s, j):
        return firsts[g] * blocks + (s + 1) * lengths[g][0] - lengths[g][j]

    def rs(g, s, j):
        half = lengths[g][j + 1]
        b = orders[s][j]
        away = pl.multiple_of(offs[g][s][j] + (1 - bit(b)) * half, 8)
        spot = spot_of(g, s, j)
        return copy_to(
            "mp", partner(b), z.at[pl.ds(away, half)], got.at[spot:spot + half],
            rs_send.at[g, s, j], rs_recv.at[g, s, j],
        )

    def reduce_step(g, j, pass_on=False):
        for s in range(2):
            if j > 0:
                half, spot = lengths[g][j], spot_of(g, s, j - 1)
                rs(g, s, j - 1).wait()
                keep = pl.ds(offs[g][s][j], half)
                z[keep, :] = z[keep, :] + got[spot:spot + half, :]
            if j < bits:
                rs(g, s, j).start()
            if pass_on:
                line_edge(g, s)

    top = rank // 2
    mine_half = pl.ds(pl.multiple_of(bit(0) * top, top), top)
    other_half = pl.ds(pl.multiple_of((1 - bit(0)) * top, top), top)

    def gram(j):
        if j == 0:
            src, dst, b = gwork.at[other_half], ggot.at[0], 0
        elif j < bits:
            src, dst, b = ghalf.at[j - 1], ggot.at[j], j
        else:
            src, dst, b = m_ref.at[mine_half], m_ref.at[mine_half], 0
        return copy_to("mp", partner(b), src, dst, g_send.at[j], g_recv.at[j])

    def gram_step(j):
        if j > 0:
            gram(j - 1).wait()
        if 0 < j <= bits:
            before = gwork[mine_half, :] if j == 1 else ghalf[j - 2]
            if j < bits:
                ghalf[j - 1] = before + ggot[j - 1]
            else:
                m_ref[mine_half, :] = before + ggot[j - 1]
        if j <= bits:
            gram(j).start()

    def share(ref, g, s):
        return ref.at[pl.ds(offs[g][s][bits], lengths[g][bits])]

    def landing(ref, g, s):
        return ref.at[g, s, pl.ds(0, lengths[g][bits])]

    def z_part(g, s):
        return copy_to("dp", inner, share(z, g, s), landing(zpart, g, s), zin_send.at[g, s], zpart_recv.at[g, s])

    def z_cross(g, s):
        return copy_to("dp", inner, share(z, g, s), landing(zcross, g, s), zin_send.at[g, s], zcross_recv.at[g, s])

    def z_tot(g, s):
        return copy_to("dp", outer, share(full, g, s), share(full, g, s), zout_send.at[g, s], ztot_recv.at[g, s])

    def line_edge(g, s):
        @pl.when(edge)
        def _():
            inward(z_cross(g, s), z_part(g, s))

    def line_in(g):
        @pl.when(jnp.logical_not(edge))
        def _():
            for s in range(2):
                z_part(g, s).wait_recv()
                mine = share(z, g, s)
                mine[...] = mine[...] + landing(zpart, g, s)[...]
                inward(z_cross(g, s), z_part(g, s))

    def line_out(g, gather):
        for s in range(2):
            @pl.when(mid)
            def _():
                z_cross(g, s).wait_recv()
                share(full, g, s)[...] = share(z, g, s)[...] + landing(zcross, g, s)[...]

            @pl.when(jnp.logical_not(mid))
            def _():
                z_tot(g, s).wait_recv()

            @pl.when(jnp.logical_not(edge))
            def _():
                z_tot(g, s).start()

            if gather:
                gather_begin(g, s)

    def ag(g, s, j):
        mine = full.at[pl.ds(offs[g][s][j + 1], lengths[g][j + 1])]
        return copy_to("mp", partner(orders[s][j]), mine, mine, ag_send.at[g, s, j], ag_recv.at[g, s, j])

    def sibling(g, s):
        b = orders[s][bits - 1]
        at = pl.multiple_of(offs[g][s][bits - 1] + (1 - bit(b)) * lengths[g][bits], 8)
        mine = full.at[pl.ds(at, lengths[g][bits])]
        return copy_to("mp", partner(orders[s][bits - 2]), mine, mine, ag_send.at[g, s, bits - 2], ag_recv.at[g, s, bits - 2])

    def direct(g, s):
        mine = share(full, g, s)
        return copy_to("mp", partner(orders[s][bits - 2]), mine, mine, ag_send.at[g, s, bits], ag_recv.at[g, s, bits])

    def gather_begin(g, s):
        ag(g, s, bits - 1).start()
        direct(g, s).start()

    def gather_step(g, k):
        for s in range(2):
            if k == 0:
                gather_begin(g, s)
            elif k == 1:
                ag(g, s, bits - 1).wait()
                sibling(g, s).start()
            elif k == 2:
                sibling(g, s).wait()
                direct(g, s).wait()
            else:
                ag(g, s, bits - k).wait()
            if 1 < k < bits:
                ag(g, s, bits - 1 - k).start()

    def work(name, g, j):
        if name == "reduce":
            reduce_step(g, j)
        elif name == "pass":
            reduce_step(g, bits, True)
        elif name == "edge":
            for s in range(2):
                line_edge(g, s)
        elif name == "in":
            line_in(g)
        elif name == "out":
            line_out(g, j)
        elif name == "gather":
            gather_step(g, j)
        elif name == "gram":
            gram_step(j)
        elif name == "eliminate":
            eliminate(m_ref, rank * j // 4, rank * (j + 1) // 4)

    at = max(count - ahead, 0)
    for when, entry in timetable(bits, count):
        if when > at:
            exchange(at, when)
            at = when
        work(*entry)

    for g in range(GROUPS):
        def sent(c, carry):
            send_part(g, c).wait_send()

            @pl.when(jnp.logical_not(edge))
            def _():
                send_tot(g, c).wait_send()

            return carry

        lax.fori_loop(0, count, sent, 0)
        for s in range(2):
            z_part(g, s).wait_send()

        @pl.when(jnp.logical_not(edge))
        def _():
            for s in range(2):
                z_tot(g, s).wait_send()


def timetable(bits, count):
    end = GROUPS * count + LAG
    final, after = GROUPS - 1, GROUPS - 2
    table = []
    for g in range(final):
        done = (g + 1) * count + LAG
        delays = [0, 2] + [2 + -(-SPANS[g] * j // (bits - 1)) for j in range(1, bits)]
        table += [(done + delay, ("reduce", g, j)) for j, delay in enumerate(delays)]
        if g < after:
            table.append((done + delays[bits] + 2, ("edge", g, 0)))
    tail = [entry for when, entry in table if when >= end and entry[1] < after]
    table = sorted((pair for pair in table if pair[0] < end), key=lambda pair: pair[0])
    begun = min(sum(entry[:2] == ("reduce", after) for _, entry in table), bits)
    table = [pair for pair in table if pair[1] != ("reduce", after, bits)]
    late = [("reduce", after, j) for j in range(begun, bits)] + [("pass", after, 0)]
    ordered = [("reduce", final, 0), ("gram", 0, 0)] + tail + late[:-1]
    ordered += [("in", 0, 0), ("reduce", final, 1), ("gram", 0, 1), late[-1], ("out", 0, 0)]
    ordered += [("in", g, 0) for g in range(1, after)]
    ordered += [("reduce", final, j) for j in range(2, bits)] + [("gram", 0, 2), ("pass", final, 0), ("gather", 0, 0)]
    ordered += [("gram", 0, j) for j in range(3, bits + 1)] + [("out", g, 1) for g in range(1, after)]
    ordered += [("in", after, 0), ("gram", 0, bits + 1), ("eliminate", 0, 0), ("gather", 0, 1), ("out", after, 1)]
    ordered += [("gather", g, 1) for g in range(1, after)] + [("eliminate", 0, 1), ("in", final, 0)]
    ordered += [("gather", 0, j) for j in range(2, bits)] + [("gather", after, 1)]
    ordered += [("gather", g, j) for g in range(1, after) for j in range(2, bits)]
    ordered += [("eliminate", 0, 2), ("gather", 0, bits)] + [("gather", after, j) for j in range(2, bits)]
    ordered += [("out", final, 1)] + [("gather", g, bits) for g in range(1, after)]
    ordered += [("eliminate", 0, 3), ("gather", final, 1), ("gather", after, bits)]
    ordered += [("gather", final, j) for j in range(2, bits + 1)]
    return table + [(end, entry) for entry in ordered]


def eliminate(m_ref, first, last):
    size = m_ref.shape[1]
    top = first // 8 * 8
    row = top + lax.broadcasted_iota(jnp.int32, (size - top, size), 0)
    lane = lax.broadcasted_iota(jnp.int32, (size - top, size), 1)
    lane1 = lax.broadcasted_iota(jnp.int32, (1, size), 1)

    def pivots(t, carry):
        k = t * UNROLL
        m = m_ref[top:, :]
        lines = [m_ref[pl.ds(k + i, 1), :] for i in range(UNROLL)]
        cols = [jnp.sum(jnp.where(lane == k + j, m, 0.0), axis=1, keepdims=True) for j in range(UNROLL)]
        corner = {
            (i, j): jnp.sum(jnp.where(lane1 == k + j, lines[i], 0.0), axis=1, keepdims=True)
            for i in range(UNROLL) for j in range(i + 1)
        }
        out = jnp.where((lane >= k) & (lane < k + UNROLL), 0.0, m)
        for j in range(UNROLL):
            scale = 1.0 / corner[j, j]
            line = jnp.where(lane1 == k + j, 1.0, lines[j])
            for i in range(j + 1, UNROLL):
                factor = corner[i, j] * scale
                lines[i] = jnp.where(lane1 == k + j, 0.0, lines[i]) - factor * line
                for l in range(j + 1, i + 1):
                    corner[i, l] = corner[i, l] - factor * corner[l, j]
            factor = cols[j] * scale
            for l in range(j + 1, UNROLL):
                cols[l] = cols[l] - factor * corner[l, j]
            out = out - factor * jnp.where((lane1 > k + j) & (lane1 < k + UNROLL), 0.0, line)
        m_ref[top:, :] = jnp.where(row >= k + UNROLL, out, m)
        for i in range(1, UNROLL):
            m_ref[pl.ds(k + i, 1), :] = lines[i]
        return carry

    lax.fori_loop(first // UNROLL, last // UNROLL, pivots, 0)


def last_kernel(n, sizes, a_ref, tot, full, m_ref, update_hbm, error_hbm, ortho, nq, update, error, update_sem, error_sem):
    rows, wide = a_ref.shape
    count, rank, rb = tot.shape
    slots, _, width = update.shape
    strips = wide // width
    m = m_ref[...]
    row = lax.broadcasted_iota(jnp.int32, (rank, rank), 0)
    lane = lax.broadcasted_iota(jnp.int32, (rank, rank), 1)
    pivots = jnp.sum(jnp.where(row == lane, m, 0.0), axis=1, keepdims=True)
    w = jnp.where(lane < row, m, jnp.where(lane == row, 1.0, 0.0)) / jnp.sqrt(pivots)

    def rows_of(r):
        return pl.ds(pl.multiple_of(r * rb, rb), rb)

    def cols_of(c):
        return pl.ds(pl.multiple_of(c * width, width), width)

    def straighten(r):
        ortho[rows_of(r), :] = jnp.dot(
            w, tot[r] / n, precision=HIGHEST, preferred_element_type=jnp.float32
        ).T.astype(jnp.bfloat16)

    def turn(c):
        for k in range(width // 128):
            spots = [sum(sizes[:g]) * (wide // 128) + (c * (width // 128) + k) * sizes[g] for g in range(GROUPS)]
            right = jnp.concatenate(
                [full[pl.ds(pl.multiple_of(spot, 8), rg), :] for spot, rg in zip(spots, sizes)], axis=0
            )
            nq[:, pl.ds(pl.multiple_of(c * width + k * 128, 128), 128)] = (
                jnp.dot(w, right, precision=HIGHEST, preferred_element_type=jnp.float32) / n
            ).astype(jnp.bfloat16)

    def write(slot, r, c):
        return (
            pltpu.make_async_copy(update.at[slot], update_hbm.at[rows_of(r), cols_of(c)], update_sem.at[slot]),
            pltpu.make_async_copy(error.at[slot], error_hbm.at[rows_of(r), cols_of(c)], error_sem.at[slot]),
        )

    def block(i, r, c):
        slot = lax.rem(i, slots)

        @pl.when(i >= slots)
        def _():
            for copy in write(slot, r, c):
                copy.wait()

        right = jnp.dot(ortho[rows_of(r), :], nq[:, cols_of(c)], preferred_element_type=jnp.float32)
        update[slot] = right
        error[slot] = (a_ref[rows_of(r), cols_of(c)].astype(jnp.float32) - right).astype(jnp.bfloat16)
        for copy in write(slot, r, c):
            copy.start()

    first = min(2, count)
    for r in range(first):
        straighten(r)

    def strip(c, carry):
        turn(c)
        for r in range(first):
            block(c * first + r, r, c)
        return carry

    lax.fori_loop(0, strips, strip, 0)

    def band(r, carry):
        straighten(r)

        def across(c, carry):
            block(r * strips + c, r, c)
            return carry

        return lax.fori_loop(0, strips, across, carry)

    lax.fori_loop(first, count, band, 0)
    for slot in range(min(slots, count * strips)):
        for copy in write(slot, 0, 0):
            copy.wait()


def on_device(accumulated, start_q):
    a = accumulated[0]
    rows, wide = a.shape
    rank = start_q.shape[1]
    n, peers = lax.axis_size("dp"), lax.axis_size("mp")
    bits = peers.bit_length() - 1
    assert peers == 1 << bits and bits >= 2 and n >= 2 and rank == 128
    count = chunks_of(rows)
    rb = rows // count
    f32, bf16 = jnp.float32, jnp.bfloat16
    vmem = pl.BlockSpec(memory_space=pltpu.VMEM)
    hbm = pl.BlockSpec(memory_space=pltpu.HBM)
    dma = pltpu.SemaphoreType.DMA
    flat = wide // 128 * rank
    sizes = (rank // GROUPS,) * GROUPS
    most = wide // 128 * max(sizes) // 2 // peers
    a_v, tot, full, lower = pl.pallas_call(
        functools.partial(factors_kernel, n, bits, count, sizes),
        out_shape=(
            pltpu.VMEM((rows, wide), bf16),
            pltpu.VMEM((count, rank, rb), f32),
            pltpu.VMEM((flat, 128), f32),
            pltpu.VMEM((rank, rank), f32),
        ),
        in_specs=[hbm, hbm],
        out_specs=(vmem,) * 4,
        scratch_shapes=[
            pltpu.VMEM((wide, rank), f32),
            pltpu.VMEM((count, rank, rb), f32),
            pltpu.VMEM((count, rank, rb), f32),
            pltpu.VMEM((count, rank, rb), f32),
            pltpu.VMEM((flat, 128), f32),
            pltpu.VMEM((flat, 128), f32),
            pltpu.VMEM((rank, rank), f32),
            pltpu.VMEM((bits - 1, rank // 2, rank), f32),
            pltpu.VMEM((bits, rank // 2, rank), f32),
            pltpu.VMEM((GROUPS, 2, most, 128), f32),
            pltpu.VMEM((GROUPS, 2, most, 128), f32),
            dma,
            dma((count,)),
        ] + [dma((GROUPS, count))] * 5 + [dma((GROUPS, 2, bits))] * 2 + [dma((GROUPS, 2, bits + 1))] * 2 + [dma((bits + 1,))] * 2
        + [dma((GROUPS, 2))] * 5,
        compiler_params=pltpu.CompilerParams(
            collective_id=0, has_side_effects=True, vmem_limit_bytes=VMEM_BYTES
        ),
        name="factors",
    )(a, pltpu.with_memory_space_constraint(start_q, pltpu.HBM))
    width = STRIP if wide % STRIP == 0 else 128
    update, error = pl.pallas_call(
        functools.partial(last_kernel, n, sizes),
        out_shape=(
            jax.ShapeDtypeStruct((rows, wide), f32),
            jax.ShapeDtypeStruct((rows, wide), bf16),
        ),
        in_specs=[vmem] * 4,
        out_specs=(hbm, hbm),
        scratch_shapes=[
            pltpu.VMEM((rows, rank), bf16),
            pltpu.VMEM((rank, wide), bf16),
            pltpu.VMEM((SLOTS, rb, width), f32),
            pltpu.VMEM((SLOTS, rb, width), bf16),
            dma((SLOTS,)),
            dma((SLOTS,)),
        ],
        compiler_params=pltpu.CompilerParams(vmem_limit_bytes=VMEM_BYTES),
        name="decompress",
    )(a_v, tot, full, lower)
    return (update, error[None])


def solution(mesh):
    placed = (P("dp", "mp", None), P())
    return jax.shard_map(
        on_device,
        mesh=mesh,
        in_specs=placed,
        out_specs=(P("mp", None), P("dp", "mp", None)),
        check_vma=False,
    )
```

```python
import functools

import jax
import jax.numpy as jnp
from jax import lax
from jax.experimental import pallas as pl
from jax.experimental.pallas import tpu as pltpu
from jax.sharding import PartitionSpec as P

MESH = pl.DeviceIdType.MESH
HIGHEST = lax.Precision.HIGHEST
GROUPS = 4
SPANS = (9, 9, 9)
STRIP = 1024
SLOTS = 4
LAG = 4
AHEAD = 4
EARLY = 2
UNROLL = 4
VMEM_BYTES = 30 * 1024 * 1024


def chunks_of(rows):
    for count in (7, 8, 14, 4, 2):
        if rows % (128 * count) == 0:
            return count
    return 1


def copy_to(axis, target, src, dst, send_sem, recv_sem):
    return pltpu.make_async_remote_copy(
        src_ref=src, dst_ref=dst, send_sem=send_sem, recv_sem=recv_sem,
        device_id={axis: target}, device_id_type=MESH,
    )


def greet_line(barrier, n, d):
    @pl.when(d > 0)
    def _():
        pl.semaphore_signal(barrier, inc=1, device_id={"dp": d - 1}, device_id_type=MESH)

    @pl.when(d < n - 1)
    def _():
        pl.semaphore_signal(barrier, inc=1, device_id={"dp": d + 1}, device_id_type=MESH)


def line_of(n, d):
    half = n // 2
    left = d < half
    inner = jnp.where(left, d + 1, d - 1)
    outer = jnp.where(left, d - 1, d + 1)
    edge = (d == 0) | (d == n - 1)
    mid = (d == half - 1) | (d == half)
    return inner, outer, edge, mid


def factors_kernel(n, bits, count, sizes, a_hbm, q_hbm, a_v, tot, full, m_ref, q_v, own, part, cross, z, got,
                   gwork, ghalf, ggot, zpart, zcross, q_sem, a_sem, in_send, out_send, part_recv,
                   cross_recv, tot_recv, rs_send, rs_recv, ag_send, ag_recv, g_send, g_recv, zin_send, zout_send,
                   zpart_recv, zcross_recv, ztot_recv):
    rows, wide = a_hbm.shape
    rank = q_hbm.shape[1]
    firsts = [sum(sizes[:g]) for g in range(GROUPS)]
    rb = rows // count
    blocks = wide // 128
    total = GROUPS * count
    d = lax.axis_index("dp")
    me = lax.axis_index("mp")
    inner, outer, edge, mid = line_of(n, d)

    def bit(b):
        return lax.rem(me // (1 << b), 2)

    def partner(b):
        return me + (1 - 2 * bit(b)) * (1 << b)

    def some_rows(c):
        return pl.ds(pl.multiple_of(c * rb, rb), rb)

    def load(c):
        return pltpu.make_async_copy(a_hbm.at[some_rows(c)], a_v.at[some_rows(c)], a_sem.at[c])

    def piece(ref, g, c):
        return ref.at[c, pl.ds(firsts[g], sizes[g])]

    def send_part(g, c):
        return copy_to("dp", inner, piece(own, g, c), piece(part, g, c), in_send.at[g, c], part_recv.at[g, c])

    def send_cross(g, c):
        return copy_to("dp", inner, piece(own, g, c), piece(cross, g, c), in_send.at[g, c], cross_recv.at[g, c])

    def send_tot(g, c):
        return copy_to("dp", outer, piece(tot, g, c), piece(tot, g, c), out_send.at[g, c], tot_recv.at[g, c])

    def inward(crossing, passing):
        @pl.when(mid)
        def _():
            crossing.start()

        @pl.when(jnp.logical_not(mid))
        def _():
            passing.start()

    load_q = pltpu.make_async_copy(q_hbm, q_v, q_sem)
    load_q.start()
    load(0).start()
    barrier = pltpu.get_barrier_semaphore()
    greet_line(barrier, n, d)
    for b in range(bits):
        pl.semaphore_signal(barrier, inc=1, device_id={"mp": partner(b)}, device_id_type=MESH)
    gwork[...] = jnp.zeros_like(gwork)
    z[...] = jnp.zeros_like(z)
    load_q.wait()
    for c in range(1, count):
        load(c).start()
    q_bf = q_v[...].astype(jnp.bfloat16)

    def front(g, c):
        @pl.when(jnp.logical_not(edge))
        def _():
            send_part(g, c).wait_recv()
            mine = piece(own, g, c)
            mine[...] = mine[...] + piece(part, g, c)[...]
            inward(send_cross(g, c), send_part(g, c))

    early = min(EARLY, count)
    ahead = max(AHEAD, count - LAG)
    for c in range(count):
        load(c).wait()
        own[c] = jnp.dot(a_v[c * rb:(c + 1) * rb, :], q_bf, preferred_element_type=jnp.float32).T
        if c == early - 1:
            pl.semaphore_wait(barrier, jnp.where(d > 0, 1, 0) + jnp.where(d < n - 1, 1, 0) + bits)
        if c >= early - 1:
            @pl.when(edge)
            def _():
                for k in range(0 if c == early - 1 else c, c + 1):
                    inward(send_cross(0, k), send_part(0, k))
        if c >= ahead:
            front(0, c - ahead)

    @pl.when(edge)
    def _():
        for g in range(1, GROUPS):
            def rest(c, carry):
                inward(send_cross(g, c), send_part(g, c))
                return carry

            lax.fori_loop(0, count, rest, 0)

    def back(g, c):
        rg = sizes[g]

        @pl.when(mid)
        def _():
            send_cross(g, c).wait_recv()
            piece(tot, g, c)[...] = piece(own, g, c)[...] + piece(cross, g, c)[...]

        @pl.when(jnp.logical_not(mid))
        def _():
            send_tot(g, c).wait_recv()

        @pl.when(jnp.logical_not(edge))
        def _():
            send_tot(g, c).start()

        mean = piece(tot, g, c)[...] / n
        high = mean.astype(jnp.bfloat16)
        low = (mean - high.astype(jnp.float32)).astype(jnp.bfloat16)
        both = jnp.concatenate([high, low], axis=0)
        step = 512 if wide % 512 == 0 else 128
        for col in range(0, wide, step):
            sums = jnp.dot(both, a_v[some_rows(c), col:col + step], preferred_element_type=jnp.float32)
            for k in range(step // 128):
                at, cols = firsts[g] * blocks + (col // 128 + k) * rg, slice(k * 128, k * 128 + 128)
                z[at:at + rg, :] += sums[:rg, cols] + sums[rg:, cols]

        if g == GROUPS - 1:
            whole = tot[c] / n
            gwork[...] += lax.dot_general(
                whole, whole, (((1,), (1,)), ((), ())), precision=HIGHEST,
                preferred_element_type=jnp.float32,
            )

    def exchange(first, last):
        marks = [g * count + shift for g in range(GROUPS + 1) for shift in (0, LAG)]
        cuts = sorted({first, last} | {mark for mark in marks if first < mark < last})
        for low, high in zip(cuts, cuts[1:]):
            def step(t, carry):
                if low < total:
                    front(low // count, t - low // count * count)
                if low >= LAG:
                    g = (low - LAG) // count
                    back(g, t - LAG - g * count)
                return carry

            lax.fori_loop(low, high, step, 0)

    orders = (tuple(range(bits)), (0,) + tuple(range(bits - 1, 0, -1)))
    lengths = [[blocks * rg // 2 >> j for j in range(bits + 1)] for rg in sizes]
    offs = []
    for g in range(GROUPS):
        offs.append([])
        for s in range(2):
            at = [firsts[g] * blocks + s * lengths[g][0]]
            for j in range(bits):
                at.append(pl.multiple_of(at[j] + bit(orders[s][j]) * lengths[g][j + 1], 8))
            offs[g].append(at)

    def spot_of(g, s, j):
        return firsts[g] * blocks + (s + 1) * lengths[g][0] - lengths[g][j]

    def rs(g, s, j):
        half = lengths[g][j + 1]
        b = orders[s][j]
        away = pl.multiple_of(offs[g][s][j] + (1 - bit(b)) * half, 8)
        spot = spot_of(g, s, j)
        return copy_to(
            "mp", partner(b), z.at[pl.ds(away, half)], got.at[spot:spot + half],
            rs_send.at[g, s, j], rs_recv.at[g, s, j],
        )

    def reduce_step(g, j, pass_on=False):
        for s in range(2):
            if j > 0:
                half, spot = lengths[g][j], spot_of(g, s, j - 1)
                rs(g, s, j - 1).wait()
                keep = pl.ds(offs[g][s][j], half)
                z[keep, :] = z[keep, :] + got[spot:spot + half, :]
            if j < bits:
                rs(g, s, j).start()
            if pass_on:
                line_edge(g, s)

    top = rank // 2
    mine_half = pl.ds(pl.multiple_of(bit(0) * top, top), top)
    other_half = pl.ds(pl.multiple_of((1 - bit(0)) * top, top), top)

    def gram(j):
        if j == 0:
            src, dst, b = gwork.at[other_half], ggot.at[0], 0
        elif j < bits:
            src, dst, b = ghalf.at[j - 1], ggot.at[j], j
        else:
            src, dst, b = m_ref.at[mine_half], m_ref.at[mine_half], 0
        return copy_to("mp", partner(b), src, dst, g_send.at[j], g_recv.at[j])

    def gram_step(j):
        if j > 0:
            gram(j - 1).wait()
        if 0 < j <= bits:
            before = gwork[mine_half, :] if j == 1 else ghalf[j - 2]
            if j < bits:
                ghalf[j - 1] = before + ggot[j - 1]
            else:
                m_ref[mine_half, :] = before + ggot[j - 1]
        if j <= bits:
            gram(j).start()

    def share(ref, g, s):
        return ref.at[pl.ds(offs[g][s][bits], lengths[g][bits])]

    def landing(ref, g, s):
        return ref.at[g, s, pl.ds(0, lengths[g][bits])]

    def z_part(g, s):
        return copy_to("dp", inner, share(z, g, s), landing(zpart, g, s), zin_send.at[g, s], zpart_recv.at[g, s])

    def z_cross(g, s):
        return copy_to("dp", inner, share(z, g, s), landing(zcross, g, s), zin_send.at[g, s], zcross_recv.at[g, s])

    def z_tot(g, s):
        return copy_to("dp", outer, share(full, g, s), share(full, g, s), zout_send.at[g, s], ztot_recv.at[g, s])

    def line_edge(g, s):
        @pl.when(edge)
        def _():
            inward(z_cross(g, s), z_part(g, s))

    def line_in(g):
        @pl.when(jnp.logical_not(edge))
        def _():
            for s in range(2):
                z_part(g, s).wait_recv()
                mine = share(z, g, s)
                mine[...] = mine[...] + landing(zpart, g, s)[...]
                inward(z_cross(g, s), z_part(g, s))

    def line_out(g, gather):
        for s in range(2):
            @pl.when(mid)
            def _():
                z_cross(g, s).wait_recv()
                share(full, g, s)[...] = share(z, g, s)[...] + landing(zcross, g, s)[...]

            @pl.when(jnp.logical_not(mid))
            def _():
                z_tot(g, s).wait_recv()

            @pl.when(jnp.logical_not(edge))
            def _():
                z_tot(g, s).start()

            if gather:
                gather_begin(g, s)

    def ag(g, s, j):
        mine = full.at[pl.ds(offs[g][s][j + 1], lengths[g][j + 1])]
        return copy_to("mp", partner(orders[s][j]), mine, mine, ag_send.at[g, s, j], ag_recv.at[g, s, j])

    def sibling(g, s):
        b = orders[s][bits - 1]
        at = pl.multiple_of(offs[g][s][bits - 1] + (1 - bit(b)) * lengths[g][bits], 8)
        mine = full.at[pl.ds(at, lengths[g][bits])]
        return copy_to("mp", partner(orders[s][bits - 2]), mine, mine, ag_send.at[g, s, bits - 2], ag_recv.at[g, s, bits - 2])

    def direct(g, s):
        mine = share(full, g, s)
        return copy_to("mp", partner(orders[s][bits - 2]), mine, mine, ag_send.at[g, s, bits], ag_recv.at[g, s, bits])

    def gather_begin(g, s):
        ag(g, s, bits - 1).start()
        direct(g, s).start()

    def gather_step(g, k):
        for s in range(2):
            if k == 0:
                gather_begin(g, s)
            elif k == 1:
                ag(g, s, bits - 1).wait()
                sibling(g, s).start()
            elif k == 2:
                sibling(g, s).wait()
                direct(g, s).wait()
            else:
                ag(g, s, bits - k).wait()
            if 1 < k < bits:
                ag(g, s, bits - 1 - k).start()

    def work(name, g, j):
        if name == "reduce":
            reduce_step(g, j)
        elif name == "pass":
            reduce_step(g, bits, True)
        elif name == "edge":
            for s in range(2):
                line_edge(g, s)
        elif name == "in":
            line_in(g)
        elif name == "out":
            line_out(g, j)
        elif name == "gather":
            gather_step(g, j)
        elif name == "gram":
            gram_step(j)
        elif name == "eliminate":
            eliminate(m_ref, rank * j // 4, rank * (j + 1) // 4)

    at = max(count - ahead, 0)
    for when, entry in timetable(bits, count):
        if when > at:
            exchange(at, when)
            at = when
        work(*entry)

    for g in range(GROUPS):
        def sent(c, carry):
            send_part(g, c).wait_send()

            @pl.when(jnp.logical_not(edge))
            def _():
                send_tot(g, c).wait_send()

            return carry

        lax.fori_loop(0, count, sent, 0)
        for s in range(2):
            z_part(g, s).wait_send()

        @pl.when(jnp.logical_not(edge))
        def _():
            for s in range(2):
                z_tot(g, s).wait_send()


def timetable(bits, count):
    end = GROUPS * count + LAG
    final, after = GROUPS - 1, GROUPS - 2
    table = []
    for g in range(final):
        done = (g + 1) * count + LAG
        delays = [0, 2] + [2 + -(-SPANS[g] * j // (bits - 1)) for j in range(1, bits)]
        table += [(done + delay, ("reduce", g, j)) for j, delay in enumerate(delays)]
        if g < after:
            table.append((done + delays[bits] + 2, ("edge", g, 0)))
    tail = [entry for when, entry in table if when >= end and entry[1] < after]
    table = sorted((pair for pair in table if pair[0] < end), key=lambda pair: pair[0])
    begun = min(sum(entry[:2] == ("reduce", after) for _, entry in table), bits)
    table = [pair for pair in table if pair[1] != ("reduce", after, bits)]
    late = [("reduce", after, j) for j in range(begun, bits)] + [("pass", after, 0)]
    ordered = [("reduce", final, 0), ("gram", 0, 0)] + tail + late[:-1]
    ordered += [("in", 0, 0), ("reduce", final, 1), ("gram", 0, 1), late[-1], ("out", 0, 1)]
    ordered += [("in", g, 0) for g in range(1, after)]
    ordered += [("reduce", final, j) for j in range(2, bits)] + [("gram", 0, 2), ("pass", final, 0)]
    ordered += [("gram", 0, j) for j in range(3, bits + 1)] + [("out", g, 1) for g in range(1, after)]
    ordered += [("in", after, 0), ("gram", 0, bits + 1), ("eliminate", 0, 0), ("gather", 0, 1), ("out", after, 1)]
    ordered += [("gather", g, 1) for g in range(1, after)] + [("eliminate", 0, 1), ("in", final, 0)]
    ordered += [("gather", 0, j) for j in range(2, bits)] + [("gather", after, 1)]
    ordered += [("gather", g, j) for g in range(1, after) for j in range(2, bits)]
    ordered += [("eliminate", 0, 2), ("gather", 0, bits)] + [("gather", after, j) for j in range(2, bits)]
    ordered += [("out", final, 1)] + [("gather", g, bits) for g in range(1, after)]
    ordered += [("eliminate", 0, 3), ("gather", final, 1), ("gather", after, bits)]
    ordered += [("gather", final, j) for j in range(2, bits + 1)]
    return table + [(end, entry) for entry in ordered]


def eliminate(m_ref, first, last):
    size = m_ref.shape[1]
    top = first // 8 * 8
    row = top + lax.broadcasted_iota(jnp.int32, (size - top, size), 0)
    lane = lax.broadcasted_iota(jnp.int32, (size - top, size), 1)
    lane1 = lax.broadcasted_iota(jnp.int32, (1, size), 1)

    def pivots(t, carry):
        k = t * UNROLL
        m = m_ref[top:, :]
        lines = [m_ref[pl.ds(k + i, 1), :] for i in range(UNROLL)]
        cols = [jnp.sum(jnp.where(lane == k + j, m, 0.0), axis=1, keepdims=True) for j in range(UNROLL)]
        corner = {
            (i, j): jnp.sum(jnp.where(lane1 == k + j, lines[i], 0.0), axis=1, keepdims=True)
            for i in range(UNROLL) for j in range(i + 1)
        }
        out = jnp.where((lane >= k) & (lane < k + UNROLL), 0.0, m)
        for j in range(UNROLL):
            scale = 1.0 / corner[j, j]
            line = jnp.where(lane1 == k + j, 1.0, lines[j])
            for i in range(j + 1, UNROLL):
                factor = corner[i, j] * scale
                lines[i] = jnp.where(lane1 == k + j, 0.0, lines[i]) - factor * line
                for l in range(j + 1, i + 1):
                    corner[i, l] = corner[i, l] - factor * corner[l, j]
            factor = cols[j] * scale
            for l in range(j + 1, UNROLL):
                cols[l] = cols[l] - factor * corner[l, j]
            out = out - factor * jnp.where((lane1 > k + j) & (lane1 < k + UNROLL), 0.0, line)
        m_ref[top:, :] = jnp.where(row >= k + UNROLL, out, m)
        for i in range(1, UNROLL):
            m_ref[pl.ds(k + i, 1), :] = lines[i]
        return carry

    lax.fori_loop(first // UNROLL, last // UNROLL, pivots, 0)


def last_kernel(n, sizes, a_ref, tot, full, m_ref, update_hbm, error_hbm, ortho, nq, update, error, update_sem, error_sem):
    rows, wide = a_ref.shape
    count, rank, rb = tot.shape
    slots, _, width = update.shape
    strips = wide // width
    m = m_ref[...]
    row = lax.broadcasted_iota(jnp.int32, (rank, rank), 0)
    lane = lax.broadcasted_iota(jnp.int32, (rank, rank), 1)
    pivots = jnp.sum(jnp.where(row == lane, m, 0.0), axis=1, keepdims=True)
    w = jnp.where(lane < row, m, jnp.where(lane == row, 1.0, 0.0)) / jnp.sqrt(pivots)

    def rows_of(r):
        return pl.ds(pl.multiple_of(r * rb, rb), rb)

    def cols_of(c):
        return pl.ds(pl.multiple_of(c * width, width), width)

    def straighten(r):
        ortho[rows_of(r), :] = jnp.dot(
            w, tot[r] / n, precision=HIGHEST, preferred_element_type=jnp.float32
        ).T.astype(jnp.bfloat16)

    def turn(c):
        for k in range(width // 128):
            spots = [sum(sizes[:g]) * (wide // 128) + (c * (width // 128) + k) * sizes[g] for g in range(GROUPS)]
            right = jnp.concatenate(
                [full[pl.ds(pl.multiple_of(spot, 8), rg), :] for spot, rg in zip(spots, sizes)], axis=0
            )
            nq[:, pl.ds(pl.multiple_of(c * width + k * 128, 128), 128)] = (
                jnp.dot(w, right, precision=HIGHEST, preferred_element_type=jnp.float32) / n
            ).astype(jnp.bfloat16)

    def write(slot, r, c):
        return (
            pltpu.make_async_copy(update.at[slot], update_hbm.at[rows_of(r), cols_of(c)], update_sem.at[slot]),
            pltpu.make_async_copy(error.at[slot], error_hbm.at[rows_of(r), cols_of(c)], error_sem.at[slot]),
        )

    def block(i, r, c):
        slot = lax.rem(i, slots)

        @pl.when(i >= slots)
        def _():
            for copy in write(slot, r, c):
                copy.wait()

        right = jnp.dot(ortho[rows_of(r), :], nq[:, cols_of(c)], preferred_element_type=jnp.float32)
        update[slot] = right
        error[slot] = (a_ref[rows_of(r), cols_of(c)].astype(jnp.float32) - right).astype(jnp.bfloat16)
        for copy in write(slot, r, c):
            copy.start()

    first = min(2, count)
    for r in range(first):
        straighten(r)

    def strip(c, carry):
        turn(c)
        for r in range(first):
            block(c * first + r, r, c)
        return carry

    lax.fori_loop(0, strips, strip, 0)

    def band(r, carry):
        straighten(r)

        def across(c, carry):
            block(r * strips + c, r, c)
            return carry

        return lax.fori_loop(0, strips, across, carry)

    lax.fori_loop(first, count, band, 0)
    for slot in range(min(slots, count * strips)):
        for copy in write(slot, 0, 0):
            copy.wait()


def on_device(accumulated, start_q):
    a = accumulated[0]
    rows, wide = a.shape
    rank = start_q.shape[1]
    n, peers = lax.axis_size("dp"), lax.axis_size("mp")
    bits = peers.bit_length() - 1
    assert peers == 1 << bits and bits >= 2 and n >= 2 and rank == 128
    count = chunks_of(rows)
    rb = rows // count
    f32, bf16 = jnp.float32, jnp.bfloat16
    vmem = pl.BlockSpec(memory_space=pltpu.VMEM)
    hbm = pl.BlockSpec(memory_space=pltpu.HBM)
    dma = pltpu.SemaphoreType.DMA
    flat = wide // 128 * rank
    sizes = (rank // GROUPS,) * GROUPS
    most = wide // 128 * max(sizes) // 2 // peers
    a_v, tot, full, lower = pl.pallas_call(
        functools.partial(factors_kernel, n, bits, count, sizes),
        out_shape=(
            pltpu.VMEM((rows, wide), bf16),
            pltpu.VMEM((count, rank, rb), f32),
            pltpu.VMEM((flat, 128), f32),
            pltpu.VMEM((rank, rank), f32),
        ),
        in_specs=[hbm, hbm],
        out_specs=(vmem,) * 4,
        scratch_shapes=[
            pltpu.VMEM((wide, rank), f32),
            pltpu.VMEM((count, rank, rb), f32),
            pltpu.VMEM((count, rank, rb), f32),
            pltpu.VMEM((count, rank, rb), f32),
            pltpu.VMEM((flat, 128), f32),
            pltpu.VMEM((flat, 128), f32),
            pltpu.VMEM((rank, rank), f32),
            pltpu.VMEM((bits - 1, rank // 2, rank), f32),
            pltpu.VMEM((bits, rank // 2, rank), f32),
            pltpu.VMEM((GROUPS, 2, most, 128), f32),
            pltpu.VMEM((GROUPS, 2, most, 128), f32),
            dma,
            dma((count,)),
        ] + [dma((GROUPS, count))] * 5 + [dma((GROUPS, 2, bits))] * 2 + [dma((GROUPS, 2, bits + 1))] * 2 + [dma((bits + 1,))] * 2
        + [dma((GROUPS, 2))] * 5,
        compiler_params=pltpu.CompilerParams(
            collective_id=0, has_side_effects=True, vmem_limit_bytes=VMEM_BYTES
        ),
        name="factors",
    )(a, pltpu.with_memory_space_constraint(start_q, pltpu.HBM))
    width = STRIP if wide % STRIP == 0 else 128
    update, error = pl.pallas_call(
        functools.partial(last_kernel, n, sizes),
        out_shape=(
            jax.ShapeDtypeStruct((rows, wide), f32),
            jax.ShapeDtypeStruct((rows, wide), bf16),
        ),
        in_specs=[vmem] * 4,
        out_specs=(hbm, hbm),
        scratch_shapes=[
            pltpu.VMEM((rows, rank), bf16),
            pltpu.VMEM((rank, wide), bf16),
            pltpu.VMEM((SLOTS, rb, width), f32),
            pltpu.VMEM((SLOTS, rb, width), bf16),
            dma((SLOTS,)),
            dma((SLOTS,)),
        ],
        compiler_params=pltpu.CompilerParams(vmem_limit_bytes=VMEM_BYTES),
        name="decompress",
    )(a_v, tot, full, lower)
    return (update, error[None])


def solution(mesh):
    placed = (P("dp", "mp", None), P())
    return jax.shard_map(
        on_device,
        mesh=mesh,
        in_specs=placed,
        out_specs=(P("mp", None), P("dp", "mp", None)),
        check_vma=False,
    )
```
